512 devices in a mesh: adapter: 32 (over z, core), tensor: 16 (over x, y).
Axes of the slice: x: 4, y: 4, z: 16, core: 2. Of those that a mesh axis runs over, the one named last changes fastest.
Arguments:
- attn_output: bfloat16 [8192, 8192], P('adapter', 'tensor'), may hold values from -6 to 6
- output_grad: bfloat16 [8192, 8192], P(('adapter', 'tensor')), may hold values from -6 to 6
- adapter_ids: int32 [8192], P('adapter'), may hold values from 0 to 1023, as said below
- base_weight: bfloat16 [8192, 8192], P('tensor', 'adapter'), may hold values from -0.0625 to 0.0625
- adapter_down: bfloat16 [8192, 16384], P('tensor', 'adapter'), may hold values from -0.1796875 to 0.1796875
- adapter_up: bfloat16 [16384, 8192], P('adapter', 'tensor'), may hold values from -0.0625 to 0.0625
Outputs:
- attention_output_gradient: bfloat16 [8192, 8192], P('adapter', 'tensor')
- down_grad: float32 [8192, 16384], P('tensor', 'adapter')
- up_grad: float32 [16384, 8192], P('adapter', 'tensor')
The draws below stay inside these ranges and needn't reach their ends.
Inputs may be any that keep to these rules, and one draw needn't show every extreme that they name: `adapter_ids`: the 256 tokens of each index of adapter form one block; the owner of adapter a is a // 32. At most 20 tokens of a block have adapters of one owner, and one owner, drawn from the seed, gets exactly 20 tokens of every block.
All inputs are finite; a program needn't handle non-finite values.
Results may differ from the reference program's by a relative error of at most 0.007.
Values may be sent and summed in bfloat16 or wider, within the bound.
A program may use at most 64 MiB of HBM per device.

```python
import jax
import jax.numpy as jnp
from jax import lax

MODEL_WIDTH = 8192
ADAPTER_RANK = 16
ADP_DEV = 32
TOK_DEV = 256
TOKEN_TOTAL = 8192
ADAPTERS = 1024
CAP = 20
SLOTS = 640


def draw_adapter_ids(key, part):
    owners = ADAPTERS // ADP_DEV
    busy_key, row_key, local_key = jax.random.split(jax.random.fold_in(key, 17), 3)
    busiest = jax.random.randint(busy_key, (), 0, owners)

    def one_block(block_key):
        pick_key, order_key = jax.random.split(block_key)
        chosen = jax.random.permutation(pick_key, (owners - 1) * CAP)[:TOK_DEV - CAP]
        others = (chosen // CAP).astype(jnp.int32)
        others = others + (others >= busiest).astype(jnp.int32)
        all_rows = jnp.concatenate([jnp.full((CAP,), busiest, jnp.int32), others])
        return jax.random.permutation(order_key, all_rows)
    block_keys = jax.random.split(row_key, owners)
    owner_ids = jax.vmap(one_block)(block_keys).reshape(-1)
    local_ids = jax.random.randint(local_key, (TOKEN_TOTAL,), 0, ADP_DEV)
    return (owner_ids * ADP_DEV + local_ids).astype(jnp.int32)


def block_levels(stream_key, dims, shards, smallest, high):
    loudness, own = 1.0, jax.random.fold_in(stream_key, 6)
    for axis_at, parts in shards:
        draws = jnp.exp(jax.random.uniform(jax.random.fold_in(own, axis_at), (parts,), jnp.float32, smallest / len(shards), high / len(shards)))
        loudness = loudness * jnp.repeat(draws, dims[axis_at] // parts).reshape([-1 if axis == axis_at else 1 for axis in range(len(dims))])
    return loudness


def normal_values(stream_key, shape, scale, limit, cuts=(), kind=jnp.bfloat16):
    drawn = jax.random.normal(stream_key, shape, jnp.float32) * scale
    if len(cuts) > 0:
        drawn = block_levels(stream_key, shape, cuts, -0.22, 0.18) * drawn
    return jnp.clip(drawn, min=-limit, max=limit).astype(kind)


def setup_inputs(seed: int = 0) -> dict:
    keys = jax.random.split(jax.random.key(seed), 7)
    return {
        "attn_output": normal_values(keys[0], (TOKEN_TOTAL, MODEL_WIDTH), 1.0, 6.0, ((0, 32), (1, 16))),
        "output_grad": normal_values(keys[1], (TOKEN_TOTAL, MODEL_WIDTH), 1.0, 6.0, ((0, 512),)),
        "adapter_ids": draw_adapter_ids(jax.random.fold_in(keys[6], 71), 0),
        "base_weight": normal_values(keys[3], (MODEL_WIDTH, MODEL_WIDTH), MODEL_WIDTH ** -0.5, 0.0625, ((0, 16), (1, 32))),
        "adapter_down": normal_values(keys[4], (MODEL_WIDTH, ADAPTERS * ADAPTER_RANK), 0.03, 0.1796875, ((0, 16), (1, 32))),
        "adapter_up": normal_values(keys[5], (ADAPTERS * ADAPTER_RANK, MODEL_WIDTH), MODEL_WIDTH ** -0.5, 0.0625, ((0, 32), (1, 16))),
    }


ADAPTER_SCALE = 2.0


def reference(attn_output, output_grad, adapter_ids, base_weight, adapter_down, adapter_up):
    owners = ADAPTERS // ADP_DEV
    block_width = ADP_DEV * ADAPTER_RANK
    frozen_output = jnp.dot(output_grad, base_weight.T, preferred_element_type=jnp.float32)
    owner_of = (adapter_ids // ADP_DEV).astype(jnp.int32)
    local_of = (adapter_ids % ADP_DEV).astype(jnp.int32)
    sorted_token_order = jnp.argsort(owner_of, stable=True).astype(jnp.int32)
    sorted_owner = owner_of[sorted_token_order]
    sorted_local = local_of[sorted_token_order]
    sorted_inputs = attn_output[sorted_token_order]
    sorted_grads = output_grad[sorted_token_order]
    member = (owner_of[:, None] == jnp.arange(owners, dtype=jnp.int32)[None, :]).astype(jnp.int32)
    counts = jnp.sum(member, axis=0).astype(jnp.int32)
    offsets = (jnp.cumsum(counts) - counts).astype(jnp.int32)

    def one_owner(running_total, owner_index):
        leading_row = jnp.minimum(offsets[owner_index], TOKEN_TOTAL - SLOTS).astype(jnp.int32)
        rows_inputs = lax.dynamic_slice_in_dim(sorted_inputs, leading_row, SLOTS, 0)
        rows_grads = lax.dynamic_slice_in_dim(sorted_grads, leading_row, SLOTS, 0)
        rows_owner = lax.dynamic_slice_in_dim(sorted_owner, leading_row, SLOTS, 0)
        rows_local = lax.dynamic_slice_in_dim(sorted_local, leading_row, SLOTS, 0)
        down_weight_block = lax.dynamic_slice_in_dim(adapter_down, (owner_index * block_width).astype(jnp.int32), block_width, 1)
        up_block = lax.dynamic_slice_in_dim(adapter_up, (owner_index * block_width).astype(jnp.int32), block_width, 0)
        chosen = jnp.logical_and(rows_owner[:, None] == owner_index, rows_local[:, None] == jnp.arange(ADP_DEV, dtype=jnp.int32)[None, :]).astype(jnp.float32)
        spread = jnp.repeat(chosen, ADAPTER_RANK, axis=1)
        rank_inputs = (jnp.dot(rows_inputs, down_weight_block, preferred_element_type=jnp.float32) * spread).reshape(SLOTS, ADP_DEV, ADAPTER_RANK).sum(axis=1)
        rank_gradients = (jnp.dot(rows_grads, up_block.T, preferred_element_type=jnp.float32) * spread).reshape(SLOTS, ADP_DEV, ADAPTER_RANK).sum(axis=1)
        scaled_up_weight = (ADAPTER_SCALE * rank_inputs).astype(jnp.bfloat16)
        rank_gradient = (ADAPTER_SCALE * rank_gradients).astype(jnp.bfloat16)
        spread_half = spread.astype(jnp.bfloat16)
        wide_gradient = jnp.tile(rank_gradient, (1, ADP_DEV)) * spread_half
        up_wide = jnp.tile(scaled_up_weight, (1, ADP_DEV)) * spread_half
        down_part = jnp.dot(rows_inputs.T, wide_gradient, preferred_element_type=jnp.float32)
        up_part = jnp.dot(up_wide.T, rows_grads, preferred_element_type=jnp.float32)
        adapter_block = jnp.dot(wide_gradient, down_weight_block.T, preferred_element_type=jnp.float32).astype(jnp.bfloat16)
        adapter_block = lax.optimization_barrier(adapter_block).astype(jnp.float32)
        current_block = lax.dynamic_slice_in_dim(running_total, leading_row, SLOTS, 0)
        running_total = lax.dynamic_update_slice_in_dim(running_total, current_block + adapter_block, leading_row, 0)
        return running_total, (down_part, up_part)

    running_total, (down_parts, up_parts) = lax.scan(one_owner, jnp.zeros((TOKEN_TOTAL, MODEL_WIDTH), jnp.float32), jnp.arange(owners, dtype=jnp.int32))
    adapter_contribution = jnp.zeros((TOKEN_TOTAL, MODEL_WIDTH), jnp.float32).at[sorted_token_order].set(running_total)
    attention_output_gradient = (frozen_output + adapter_contribution).astype(jnp.bfloat16)
    down_grad = jnp.transpose(down_parts, (1, 0, 2)).reshape(MODEL_WIDTH, ADAPTERS * ADAPTER_RANK)
    up_grad = up_parts.reshape(ADAPTERS * ADAPTER_RANK, MODEL_WIDTH)
    return attention_output_gradient, down_grad, up_grad
```

```python
import functools

import jax
import jax.numpy as jnp
from jax import lax
from jax.experimental import pallas as pl
from jax.experimental.pallas import tpu as pltpu
from jax.sharding import PartitionSpec as P

ADAPTER_RANK = 16
ADAPTER_SCALE = 2.0
MESH = pl.DeviceIdType.MESH
ANY = pl.BlockSpec(memory_space=pl.ANY)
VMEM = pl.BlockSpec(memory_space=pltpu.VMEM)
SIDE = 4
LABEL_ROWS = 16


def remote(src, dst, send_sem, recv_sem, **where):
    return pltpu.make_async_remote_copy(
        src_ref=src,
        dst_ref=dst,
        send_sem=send_sem,
        recv_sem=recv_sem,
        device_id=where,
        device_id_type=MESH,
    )


def partner(q, chips):
    me = lax.axis_index("adapter")
    z, core = me // 2, me % 2
    i, flip = q // 2, (q + 1) % 2
    half = chips // 2
    shift = half + (1 - 2 * (i % 2)) * ((i + 1) // 2)
    return ((z + shift) % chips) * 2 + (core + flip) % 2


def signal(barrier, **where):
    pl.semaphore_signal(barrier, inc=1, device_id=where, device_id_type=MESH)


def loop(n, body):
    def step(k, carry):
        body(k)
        return carry

    lax.fori_loop(0, n, step, 0)


def exchange(owners, rows, src, dst, send_sem, recv_sem):
    me = lax.axis_index("adapter")

    def copy(q):
        to = partner(q, owners // 2)
        return remote(
            src.at[pl.ds(pl.multiple_of(to * rows, rows), rows)],
            dst.at[pl.ds(pl.multiple_of(me * rows, rows), rows)],
            send_sem.at[q],
            recv_sem.at[q],
            adapter=to,
        )

    return copy


def own_block(rows, src, dst, sem):
    me = lax.axis_index("adapter")
    mine = pl.ds(pl.multiple_of(me * rows, rows), rows)
    return pltpu.make_async_copy(src.at[mine], dst.at[mine], sem)


def greet_owners(owners, barrier):
    loop(owners - 1, lambda q: signal(barrier, adapter=partner(q, owners // 2)))


def swap_kernel(owners, rows, src, dst, send_sem, recv_sem, own_sem):
    barrier = pltpu.get_barrier_semaphore()
    greet_owners(owners, barrier)
    pl.semaphore_wait(barrier, owners - 1)
    copy = exchange(owners, rows, src, dst, send_sem, recv_sem)
    loop(owners - 1, lambda q: copy(q).start())
    own = own_block(rows, src, dst, own_sem)
    own.start()
    own.wait()
    loop(owners - 1, lambda q: copy(q).wait())


def swap(slots, owners, call):
    rows = slots.shape[0] // owners
    return pl.pallas_call(
        functools.partial(swap_kernel, owners, rows),
        out_shape=jax.ShapeDtypeStruct(slots.shape, slots.dtype),
        in_specs=[VMEM],
        out_specs=ANY,
        scratch_shapes=[
            pltpu.SemaphoreType.DMA((owners,)),
            pltpu.SemaphoreType.DMA((owners,)),
            pltpu.SemaphoreType.DMA,
        ],
        compiler_params=pltpu.CompilerParams(collective_id=call, has_side_effects=True),
    )(slots)


def first_kernel(
    owners, rows, src, labels, grad, dst, labels_out, full,
    send_sem, recv_sem, label_send, label_recv, own_sem, ring_send, ring_recv,
):
    t = lax.axis_index("tensor")
    x, y = t // SIDE, t % SIDE
    tokens, width = grad.shape
    half, quarter = width // 2, width // 4

    def at(x_at, y_at):
        return (x_at % SIDE) * SIDE + y_at % SIDE

    barrier = pltpu.get_barrier_semaphore()
    greet_owners(owners, barrier)
    for dx, dy in ((1, 0), (3, 0), (0, 1), (0, 3)):
        signal(barrier, tensor=at(x + dx, y + dy))
    pl.semaphore_wait(barrier, owners + 3)

    copy = exchange(owners, rows, src, dst, send_sem, recv_sem)
    label = exchange(owners, LABEL_ROWS, labels, labels_out, label_send, label_recv)

    def cut(block, first, size):
        return full.at[pl.ds(pl.multiple_of(block * tokens, tokens), tokens), pl.ds(first, size)]

    def mine(first, size):
        return grad.at[:, pl.ds(first, size)]

    started = []

    def send(src_ref, block, first, size, sem, to):
        c = remote(src_ref, cut(block, first, size), ring_send.at[sem], ring_recv.at[sem], tensor=to)
        c.start()
        started.append(c)
        return c

    def along(side, d, e):
        return at(x + d, y + e) if side == 0 else at(x + e, y + d)

    first_hop, second = [], [[], []]
    for side in (0, 1):
        base = side * half
        first_hop.append(
            [
                send(mine(base, half), t, base, half, side * 20, along(side, 1, 0)),
                send(mine(base, half), t, base, half, side * 20 + 1, along(side, 3, 0)),
            ]
        )
    for side in (0, 1):
        base = side * half
        second[side].append(
            [
                send(mine(base, half), t, base, half, side * 20 + 4, along(side, 0, 1)),
                send(mine(base, half), t, base, half, side * 20 + 5, along(side, 0, 3)),
            ]
        )
    loop(owners - 1, lambda q: copy(q).start())
    loop(owners - 1, lambda q: label(q).start())
    own = [
        own_block(rows, src, dst, own_sem.at[0]),
        own_block(LABEL_ROWS, labels, labels_out, own_sem.at[1]),
        pltpu.make_async_copy(grad, cut(t, 0, width), own_sem.at[2]),
    ]
    for c in own:
        c.start()
    last_hop = []
    for side in (0, 1):
        base, sem = side * half, side * 20
        a, b = first_hop[side]
        a.wait_recv()
        from_a = along(side, 3, 0)
        f1 = send(cut(from_a, base, quarter), from_a, base, quarter, sem + 2, along(side, 1, 0))
        b.wait_recv()
        from_b = along(side, 1, 0)
        f2 = send(cut(from_b, base + quarter, quarter), from_b, base + quarter, quarter, sem + 3, along(side, 3, 0))
        last_hop.append((f1, f2))
        for j, block in ((1, from_a), (2, from_b)):
            second[side].append(
                [
                    send(cut(block, base, half), block, base, half, sem + 4 + 4 * j, along(side, 0, 1)),
                    send(cut(block, base, half), block, base, half, sem + 5 + 4 * j, along(side, 0, 3)),
                ]
            )
    for side in (0, 1):
        base, sem = side * half, side * 20
        for c in last_hop[side]:
            c.wait_recv()
        block = along(side, 2, 0)
        second[side].append(
            [
                send(cut(block, base, half), block, base, half, sem + 16, along(side, 0, 1)),
                send(cut(block, base, half), block, base, half, sem + 17, along(side, 0, 3)),
            ]
        )
    final = []
    for j in range(4):
        for side in (0, 1):
            base, sem = side * half, side * 20
            d = (0, 3, 1, 2)[j]
            a, b = second[side][j]
            a.wait_recv()
            block = along(side, d, 3)
            final.append(
                send(cut(block, base, quarter), block, base, quarter, sem + 6 + 4 * j, along(side, 0, 1))
            )
            b.wait_recv()
            block = along(side, d, 1)
            final.append(
                send(
                    cut(block, base + quarter, quarter), block, base + quarter, quarter,
                    sem + 7 + 4 * j, along(side, 0, 3),
                )
            )
    for c in final:
        c.wait_recv()
    for c in started:
        c.wait_send()
    for c in own:
        c.wait()
    loop(owners - 1, lambda q: copy(q).wait())
    loop(owners - 1, lambda q: label(q).wait())


def first(slots, labels, grad, owners, call):
    members = SIDE * SIDE
    tokens, width = grad.shape
    return pl.pallas_call(
        functools.partial(first_kernel, owners, slots.shape[0] // owners),
        out_shape=[
            jax.ShapeDtypeStruct(slots.shape, slots.dtype),
            jax.ShapeDtypeStruct(labels.shape, labels.dtype),
            jax.ShapeDtypeStruct((members * tokens, width), grad.dtype),
        ],
        in_specs=[VMEM] * 3,
        out_specs=[ANY] * 3,
        scratch_shapes=[
            pltpu.SemaphoreType.DMA((owners,)),
            pltpu.SemaphoreType.DMA((owners,)),
            pltpu.SemaphoreType.DMA((owners,)),
            pltpu.SemaphoreType.DMA((owners,)),
            pltpu.SemaphoreType.DMA((3,)),
            pltpu.SemaphoreType.DMA((40,)),
            pltpu.SemaphoreType.DMA((40,)),
        ],
        compiler_params=pltpu.CompilerParams(collective_id=call, has_side_effects=True),
    )(slots, labels, grad)


def weight_kernel(
    owners, members, weight, part, full, parts, ring_send, ring_recv, twin_send, twin_recv, part_send, part_recv, own_sem,
):
    chips = owners // 2
    me, t = lax.axis_index("adapter"), lax.axis_index("tensor")
    z, core = me // 2, me % 2
    depth, width = weight.shape
    rows = depth // 2
    right, left, twin = ((z + 1) % chips) * 2 + core, ((z + chips - 1) % chips) * 2 + core, z * 2 + 1 - core
    part_rows = part.shape[0]
    far = chips // 2

    barrier = pltpu.get_barrier_semaphore()
    for to in (right, left, twin):
        signal(barrier, adapter=to)
    loop(members - 1, lambda k: signal(barrier, tensor=(t + k + 1) % members))
    pl.semaphore_wait(barrier, members + 2)

    def cut(chip, h):
        column = pl.multiple_of(((chip % chips) * 2 + core) * width, width)
        return full.at[pl.ds(h * rows, rows), pl.ds(column, width)]

    def hop(s, h, way, src=None):
        chip = z + chips - s + 1 if way == 0 else z + s - 1
        return remote(
            cut(chip, h) if src is None else src,
            cut(chip, h),
            ring_send.at[s, h, way],
            ring_recv.at[s, h, way],
            adapter=right if way == 0 else left,
        )

    def pass_on(s, h, way, src=None):
        chip = z + chips - s if way == 0 else z + s
        return remote(
            cut(chip, h) if src is None else src,
            cut(chip, h),
            twin_send.at[s, h, way],
            twin_recv.at[s, h, way],
            adapter=twin,
        )

    def share(k):
        to = (t + k + 1) % members
        return remote(
            part,
            parts.at[pl.ds(pl.multiple_of(t * part_rows, part_rows), part_rows)],
            part_send.at[k],
            part_recv.at[k],
            tensor=to,
        )

    def own(h):
        return weight.at[pl.ds(h * rows, rows)]

    loop(members - 1, lambda k: share(k).start())
    for h in (0, 1):
        for way in (0, 1):
            hop(1, h, way, own(h)).start()
    for h in (0, 1):
        pass_on(0, h, 0, own(h)).start()
    keep = [
        pltpu.make_async_copy(weight, full.at[:, pl.ds(pl.multiple_of(me * width, width), width)], own_sem.at[0]),
        pltpu.make_async_copy(
            part, parts.at[pl.ds(pl.multiple_of(t * part_rows, part_rows), part_rows)], own_sem.at[1]
        ),
    ]
    for c in keep:
        c.start()

    def step(s):
        for h in (0, 1):
            for way in (0, 1):
                hop(s - 1, h, way).wait_recv()
                hop(s, h, way).start()
                pass_on(s - 1, h, way).start()

    loop(far - 2, lambda k: step(k + 2))
    for h in (0, 1):
        for way in (0, 1):
            hop(far - 1, h, way).wait_recv()
            if h == way:
                hop(far, h, way).start()
            pass_on(far - 1, h, way).start()
    for h in (0, 1):
        hop(far, h, h).wait_recv()
        pass_on(far, h, h).start()

    def finish(k):
        for h in (0, 1):
            for way in (0, 1):
                hop(k + 1, h, way).wait_send()
                pass_on(k + 1, h, way).wait()

    loop(far - 1, finish)
    for h in (0, 1):
        hop(far, h, h).wait_send()
        pass_on(far, h, h).wait()
        pass_on(0, h, 0, own(h)).wait()
    for c in keep:
        c.wait()
    loop(members - 1, lambda k: share(k).wait())


def weights(weight, part, owners, members, call):
    depth, width = weight.shape
    steps = owners // 4 + 1
    return pl.pallas_call(
        functools.partial(weight_kernel, owners, members),
        out_shape=[
            jax.ShapeDtypeStruct((depth, owners * width), weight.dtype),
            jax.ShapeDtypeStruct((members * part.shape[0], part.shape[1]), part.dtype),
        ],
        in_specs=[VMEM] * 2,
        out_specs=[ANY] * 2,
        scratch_shapes=[
            pltpu.SemaphoreType.DMA((steps, 2, 2)),
            pltpu.SemaphoreType.DMA((steps, 2, 2)),
            pltpu.SemaphoreType.DMA((steps, 2, 2)),
            pltpu.SemaphoreType.DMA((steps, 2, 2)),
            pltpu.SemaphoreType.DMA((members,)),
            pltpu.SemaphoreType.DMA((members,)),
            pltpu.SemaphoreType.DMA((2,)),
        ],
        compiler_params=pltpu.CompilerParams(collective_id=call, has_side_effects=True),
    )(weight, part)


def dot(a, b, dims):
    return lax.dot_general(a, b, (dims, ((), ())), preferred_element_type=jnp.float32)


def per_device(attn_output, output_grad, adapter_ids, base_weight, adapter_down, adapter_up):
    owners, members = lax.axis_size("adapter"), lax.axis_size("tensor")
    tok_rows, width_part = attn_output.shape
    capacity = 5 * tok_rows // (2 * owners)
    slots = owners * capacity
    per_owner = adapter_down.shape[1] // ADAPTER_RANK
    lanes = 128

    def pack(a):
        return a.reshape(slots * width_part // lanes, lanes)

    def unpack(a):
        return a.reshape(slots, width_part)

    owner_of = adapter_ids // per_owner
    local_of = adapter_ids % per_owner
    order = jnp.arange(tok_rows, dtype=jnp.int32)
    earlier = (owner_of[:, None] == owner_of[None, :]) & (order[:, None] < order[None, :])
    rank_in = jnp.sum(earlier.astype(jnp.int32), axis=0)
    slot_of = owner_of * capacity + rank_in
    place = jnp.arange(slots, dtype=jnp.int32)[:, None] == slot_of[None, :]
    place_half = place.astype(jnp.bfloat16)
    marks = jnp.sum(jnp.where(place, (local_of + 1)[None, :], 0), axis=1).reshape(owners, 1, capacity)
    marks = jnp.pad(marks.astype(jnp.bfloat16), ((0, 0), (0, LABEL_ROWS - 1), (0, lanes - capacity)))
    send_inputs = dot(place_half, attn_output, ((1,), (0,))).astype(jnp.bfloat16)
    recv_inputs, recv_marks, full_grad = first(
        pack(send_inputs), marks.reshape(owners * LABEL_ROWS, lanes), output_grad, owners, 1
    )
    recv_inputs = unpack(recv_inputs)
    recv_marks = recv_marks.reshape(owners, LABEL_ROWS, lanes)[:, 0, :capacity].reshape(1, slots)

    grad_part = lax.dynamic_slice_in_dim(full_grad, lax.axis_index("tensor") * width_part, width_part, 1)
    send_grads = dot(place_half, grad_part, ((1,), (0,))).astype(jnp.bfloat16)
    recv_grads = unpack(swap(pack(send_grads), owners, 2))

    adapter_of_row = jnp.arange(per_owner * ADAPTER_RANK, dtype=jnp.int32)[:, None] // ADAPTER_RANK
    spread = recv_marks.astype(jnp.float32) == (adapter_of_row + 1).astype(jnp.float32)

    def fold(a):
        return jnp.where(spread, a, 0.0).reshape(per_owner, ADAPTER_RANK, slots).sum(axis=0)

    low = jnp.concatenate(
        [
            fold(dot(adapter_down, recv_inputs, ((0,), (1,)))),
            fold(dot(adapter_up, recv_grads, ((1,), (1,)))),
        ],
        axis=0,
    )
    full_weight, low_parts = weights(base_weight, low, owners, members, 3)
    low = low_parts.reshape(members, 2 * ADAPTER_RANK, slots).sum(axis=0)
    low = (ADAPTER_SCALE * low).astype(jnp.bfloat16)

    def widen(a):
        return jnp.where(spread, jnp.tile(a, (per_owner, 1)), jnp.zeros((), jnp.bfloat16))

    up_wide, wide_gradient = widen(low[:ADAPTER_RANK]), widen(low[ADAPTER_RANK:])
    adapter_block = dot(wide_gradient, adapter_down, ((0,), (1,))).astype(jnp.bfloat16)
    returned = unpack(swap(pack(adapter_block), owners, 4))
    down_grad = dot(recv_inputs, wide_gradient, ((0,), (1,)))
    up_grad = dot(up_wide, recv_grads, ((1,), (0,)))
    frozen_gradient = dot(full_grad, full_weight, ((1,), (1,)))
    adapter_contribution = dot(place_half, returned, ((0,), (0,)))
    attention_output_gradient = (frozen_gradient + adapter_contribution).astype(jnp.bfloat16)
    return (attention_output_gradient, down_grad, up_grad)


def solution(mesh):
    placed = (
        P("adapter", "tensor"),
        P(("adapter", "tensor"), None),
        P("adapter"),
        P("tensor", "adapter"),
        P("tensor", "adapter"),
        P("adapter", "tensor"),
    )
    return jax.shard_map(
        per_device,
        mesh=mesh,
        in_specs=placed,
        out_specs=(P("adapter", "tensor"), P("tensor", "adapter"), P("adapter", "tensor")),
        check_vma=False,
    )
```

```python
import functools

import jax
import jax.numpy as jnp
from jax import lax
from jax.experimental import pallas as pl
from jax.experimental.pallas import tpu as pltpu
from jax.sharding import PartitionSpec as P

ADAPTER_RANK = 16
ADAPTER_SCALE = 2.0
MESH = pl.DeviceIdType.MESH
ANY = pl.BlockSpec(memory_space=pl.ANY)
VMEM = pl.BlockSpec(memory_space=pltpu.VMEM)
SIDE = 4


def remote(src, dst, send_sem, recv_sem, **where):
    return pltpu.make_async_remote_copy(
        src_ref=src,
        dst_ref=dst,
        send_sem=send_sem,
        recv_sem=recv_sem,
        device_id=where,
        device_id_type=MESH,
    )


def partner(q, chips):
    me = lax.axis_index("adapter")
    z, core = me // 2, me % 2
    i, flip = q // 2, (q + 1) % 2
    half = chips // 2
    shift = half + (1 - 2 * (i % 2)) * ((i + 1) // 2)
    return ((z + shift) % chips) * 2 + (core + flip) % 2


def dot(a, b, dims):
    return lax.dot_general(a, b, (dims, ((), ())), preferred_element_type=jnp.float32)


def signal(barrier, **where):
    pl.semaphore_signal(barrier, inc=1, device_id=where, device_id_type=MESH)


def loop(n, body):
    def step(k, carry):
        body(k)
        return carry

    lax.fori_loop(0, n, step, 0)


def exchange(owners, rows, src, dst, send_sem, recv_sem):
    me = lax.axis_index("adapter")

    def copy(q):
        to = partner(q, owners // 2)
        return remote(
            src.at[pl.ds(pl.multiple_of(to * rows, rows), rows)],
            dst.at[pl.ds(pl.multiple_of(me * rows, rows), rows)],
            send_sem.at[q],
            recv_sem.at[q],
            adapter=to,
        )

    return copy


def own_block(rows, src, dst, sem):
    me = lax.axis_index("adapter")
    mine = pl.ds(pl.multiple_of(me * rows, rows), rows)
    return pltpu.make_async_copy(src.at[mine], dst.at[mine], sem)


def greet_owners(owners, barrier):
    loop(owners - 1, lambda q: signal(barrier, adapter=partner(q, owners // 2)))


def label_kernel(
    owners, members, rows, src, marks, dst, marks_out,
    send_sem, recv_sem, away_send, away_recv, near_send, near_recv, own_sem,
):
    me, t = lax.axis_index("adapter"), lax.axis_index("tensor")
    chips = owners // 2
    z, core = me // 2, me % 2
    above, below = (z + t) % chips, (z + chips - t) % chips
    depth = marks.shape[0]

    barrier = pltpu.get_barrier_semaphore()
    greet_owners(owners, barrier)
    loop(members - 1, lambda k: signal(barrier, tensor=(t + k + 1) % members))
    pl.semaphore_wait(barrier, owners + members - 2)

    def block(first, blocks):
        return marks_out.at[pl.ds(pl.multiple_of(first * depth, depth), blocks * depth)]

    def away(flip):
        return remote(
            marks, block(me, 1), away_send.at[flip], away_recv.at[flip], adapter=above * 2 + (core + flip) % 2
        )

    def near(k):
        to = (t + k + 1) % members
        pair = block(below * 2, 2)
        return remote(pair, pair, near_send.at[k], near_recv.at[k], tensor=to)

    keep = pltpu.make_async_copy(marks, block(me, 1), own_sem.at[1])

    @pl.when(t == 0)
    def _():
        keep.start()

    @pl.when(t > 0)
    def _():
        away(0).start()

    away(1).start()
    copy = exchange(owners, rows, src, dst, send_sem, recv_sem)
    loop(owners - 1, lambda q: copy(q).start())
    own = own_block(rows, src, dst, own_sem.at[0])
    own.start()

    @pl.when(t == 0)
    def _():
        keep.wait()

    @pl.when(t > 0)
    def _():
        away(0).wait()

    away(1).wait()
    loop(members - 1, lambda k: near(k).start())
    own.wait()
    loop(members - 1, lambda k: near(k).wait())
    loop(owners - 1, lambda q: copy(q).wait())


def swap_labels(slots, marks, owners, members, call):
    return pl.pallas_call(
        functools.partial(label_kernel, owners, members, slots.shape[0] // owners),
        out_shape=[
            jax.ShapeDtypeStruct(slots.shape, slots.dtype),
            jax.ShapeDtypeStruct((owners * marks.shape[0], marks.shape[1]), marks.dtype),
        ],
        in_specs=[VMEM] * 2,
        out_specs=[ANY] * 2,
        scratch_shapes=[
            pltpu.SemaphoreType.DMA((owners,)),
            pltpu.SemaphoreType.DMA((owners,)),
            pltpu.SemaphoreType.DMA((2,)),
            pltpu.SemaphoreType.DMA((2,)),
            pltpu.SemaphoreType.DMA((members,)),
            pltpu.SemaphoreType.DMA((members,)),
            pltpu.SemaphoreType.DMA((2,)),
        ],
        compiler_params=pltpu.CompilerParams(collective_id=call, has_side_effects=True),
    )(slots, marks)


def last_kernel(
    owners, rows, src, grad, weight, dst, product, send_sem, recv_sem, own_sem, grad_held, weight_held, load_sem,
):
    barrier = pltpu.get_barrier_semaphore()
    greet_owners(owners, barrier)
    pl.semaphore_wait(barrier, owners - 1)
    copy = exchange(owners, rows, src, dst, send_sem, recv_sem)
    loop(owners - 1, lambda q: copy(q).start())
    own = own_block(rows, src, dst, own_sem)
    own.start()
    steps = load_sem.shape[0]
    width = grad.shape[1] // steps

    def part(k):
        return pl.ds(pl.multiple_of(k * width, width), width)

    def load(k):
        return (
            pltpu.make_async_copy(grad.at[:, part(k)], grad_held.at[:, part(k)], load_sem.at[k, 0]),
            pltpu.make_async_copy(weight.at[:, part(k)], weight_held.at[:, part(k)], load_sem.at[k, 1]),
        )

    def fetch(k):
        for c in load(k):
            c.start()

    def step(k):
        for c in load(k):
            c.wait()
        product[...] += dot(grad_held[:, part(k)], weight_held[:, part(k)], ((1,), (1,)))

    loop(steps, fetch)
    product[...] = jnp.zeros_like(product)
    loop(steps, step)
    own.wait()
    loop(owners - 1, lambda q: copy(q).wait())


def last(slots, grad, weight, owners, call):
    steps = 8
    return pl.pallas_call(
        functools.partial(last_kernel, owners, slots.shape[0] // owners),
        out_shape=[
            jax.ShapeDtypeStruct(slots.shape, slots.dtype),
            jax.ShapeDtypeStruct((grad.shape[0], weight.shape[0]), jnp.float32),
        ],
        in_specs=[VMEM, ANY, ANY],
        out_specs=[ANY, VMEM],
        scratch_shapes=[
            pltpu.SemaphoreType.DMA((owners,)),
            pltpu.SemaphoreType.DMA((owners,)),
            pltpu.SemaphoreType.DMA,
            pltpu.VMEM(grad.shape, grad.dtype),
            pltpu.VMEM(weight.shape, weight.dtype),
            pltpu.SemaphoreType.DMA((steps, 2)),
        ],
        compiler_params=pltpu.CompilerParams(
            collective_id=call, has_side_effects=True, vmem_limit_bytes=32 * 1024 * 1024
        ),
    )(slots, grad, weight)


def first_kernel(
    owners, rows, src, grad, dst, full, send_sem, recv_sem, own_sem, ring_send, ring_recv,
):
    t = lax.axis_index("tensor")
    x, y = t // SIDE, t % SIDE
    tokens, width = grad.shape
    half, quarter = width // 2, width // 4

    def at(x_at, y_at):
        return (x_at % SIDE) * SIDE + y_at % SIDE

    barrier = pltpu.get_barrier_semaphore()
    greet_owners(owners, barrier)
    for dx, dy in ((1, 0), (3, 0), (0, 1), (0, 3)):
        signal(barrier, tensor=at(x + dx, y + dy))
    pl.semaphore_wait(barrier, owners + 3)

    copy = exchange(owners, rows, src, dst, send_sem, recv_sem)

    def cut(block, first, size):
        return full.at[pl.ds(pl.multiple_of(block * tokens, tokens), tokens), pl.ds(first, size)]

    def mine(first, size):
        return grad.at[:, pl.ds(first, size)]

    started = []

    def send(src_ref, block, first, size, sem, to):
        c = remote(src_ref, cut(block, first, size), ring_send.at[sem], ring_recv.at[sem], tensor=to)
        c.start()
        started.append(c)
        return c

    def along(side, d, e):
        return at(x + d, y + e) if side == 0 else at(x + e, y + d)

    first_hop, second = [], [[], []]
    for side in (0, 1):
        base = side * half
        first_hop.append(
            [
                send(mine(base, half), t, base, half, side * 20, along(side, 1, 0)),
                send(mine(base, half), t, base, half, side * 20 + 1, along(side, 3, 0)),
            ]
        )
    for side in (0, 1):
        base = side * half
        second[side].append(
            [
                send(mine(base, half), t, base, half, side * 20 + 4, along(side, 0, 1)),
                send(mine(base, half), t, base, half, side * 20 + 5, along(side, 0, 3)),
            ]
        )
    loop(owners - 1, lambda q: copy(q).start())
    own = [
        own_block(rows, src, dst, own_sem.at[0]),
        pltpu.make_async_copy(grad, cut(t, 0, width), own_sem.at[1]),
    ]
    for c in own:
        c.start()
    last_hop = []
    for side in (0, 1):
        base, sem = side * half, side * 20
        a, b = first_hop[side]
        a.wait_recv()
        from_a = along(side, 3, 0)
        f1 = send(cut(from_a, base, quarter), from_a, base, quarter, sem + 2, along(side, 1, 0))
        b.wait_recv()
        from_b = along(side, 1, 0)
        f2 = send(cut(from_b, base + quarter, quarter), from_b, base + quarter, quarter, sem + 3, along(side, 3, 0))
        last_hop.append((f1, f2))
        for j, block in ((1, from_a), (2, from_b)):
            second[side].append(
                [
                    send(cut(block, base, half), block, base, half, sem + 4 + 4 * j, along(side, 0, 1)),
                    send(cut(block, base, half), block, base, half, sem + 5 + 4 * j, along(side, 0, 3)),
                ]
            )
    for side in (0, 1):
        base, sem = side * half, side * 20
        for c in last_hop[side]:
            c.wait_recv()
        block = along(side, 2, 0)
        second[side].append(
            [
                send(cut(block, base, half), block, base, half, sem + 16, along(side, 0, 1)),
                send(cut(block, base, half), block, base, half, sem + 17, along(side, 0, 3)),
            ]
        )
    final = []
    for j in range(4):
        for side in (0, 1):
            base, sem = side * half, side * 20
            d = (0, 3, 1, 2)[j]
            a, b = second[side][j]
            a.wait_recv()
            block = along(side, d, 3)
            final.append(
                send(cut(block, base, quarter), block, base, quarter, sem + 6 + 4 * j, along(side, 0, 1))
            )
            b.wait_recv()
            block = along(side, d, 1)
            final.append(
                send(
                    cut(block, base + quarter, quarter), block, base + quarter, quarter,
                    sem + 7 + 4 * j, along(side, 0, 3),
                )
            )
    for c in final:
        c.wait_recv()
    for c in started:
        c.wait_send()
    for c in own:
        c.wait()
    loop(owners - 1, lambda q: copy(q).wait())


def first(slots, grad, owners, call):
    members = SIDE * SIDE
    tokens, width = grad.shape
    return pl.pallas_call(
        functools.partial(first_kernel, owners, slots.shape[0] // owners),
        out_shape=[
            jax.ShapeDtypeStruct(slots.shape, slots.dtype),
            jax.ShapeDtypeStruct((members * tokens, width), grad.dtype),
        ],
        in_specs=[VMEM] * 2,
        out_specs=[ANY] * 2,
        scratch_shapes=[
            pltpu.SemaphoreType.DMA((owners,)),
            pltpu.SemaphoreType.DMA((owners,)),
            pltpu.SemaphoreType.DMA((2,)),
            pltpu.SemaphoreType.DMA((40,)),
            pltpu.SemaphoreType.DMA((40,)),
        ],
        compiler_params=pltpu.CompilerParams(collective_id=call, has_side_effects=True),
    )(slots, grad)


def weight_kernel(
    owners, members, weight, part, full, parts, ring_send, ring_recv, twin_send, twin_recv, part_send, part_recv, own_sem,
):
    chips = owners // 2
    me, t = lax.axis_index("adapter"), lax.axis_index("tensor")
    z, core = me // 2, me % 2
    depth, width = weight.shape
    rows = depth // 2
    right, left, twin = ((z + 1) % chips) * 2 + core, ((z + chips - 1) % chips) * 2 + core, z * 2 + 1 - core
    part_rows = part.shape[0]
    far = chips // 2

    barrier = pltpu.get_barrier_semaphore()
    for to in (right, left, twin):
        signal(barrier, adapter=to)
    loop(members - 1, lambda k: signal(barrier, tensor=(t + k + 1) % members))
    pl.semaphore_wait(barrier, members + 2)

    def cut(chip, h):
        column = pl.multiple_of(((chip % chips) * 2 + core) * width, width)
        return full.at[pl.ds(h * rows, rows), pl.ds(column, width)]

    def hop(s, h, way, src=None):
        chip = z + chips - s + 1 if way == 0 else z + s - 1
        return remote(
            cut(chip, h) if src is None else src,
            cut(chip, h),
            ring_send.at[s, h, way],
            ring_recv.at[s, h, way],
            adapter=right if way == 0 else left,
        )

    def pass_on(s, h, way, src=None):
        chip = z + chips - s if way == 0 else z + s
        return remote(
            cut(chip, h) if src is None else src,
            cut(chip, h),
            twin_send.at[s, h, way],
            twin_recv.at[s, h, way],
            adapter=twin,
        )

    def share(k):
        to = (t + k + 1) % members
        return remote(
            part,
            parts.at[pl.ds(pl.multiple_of(t * part_rows, part_rows), part_rows)],
            part_send.at[k],
            part_recv.at[k],
            tensor=to,
        )

    def own(h):
        return weight.at[pl.ds(h * rows, rows)]

    loop(members - 1, lambda k: share(k).start())
    for h in (0, 1):
        for way in (0, 1):
            hop(1, h, way, own(h)).start()
    for h in (0, 1):
        pass_on(0, h, 0, own(h)).start()
    keep = [
        pltpu.make_async_copy(weight, full.at[:, pl.ds(pl.multiple_of(me * width, width), width)], own_sem.at[0]),
        pltpu.make_async_copy(
            part, parts.at[pl.ds(pl.multiple_of(t * part_rows, part_rows), part_rows)], own_sem.at[1]
        ),
    ]
    for c in keep:
        c.start()

    def step(s):
        for h in (0, 1):
            for way in (0, 1):
                hop(s - 1, h, way).wait_recv()
                hop(s, h, way).start()
                pass_on(s - 1, h, way).start()

    loop(far - 2, lambda k: step(k + 2))
    for h in (0, 1):
        for way in (0, 1):
            hop(far - 1, h, way).wait_recv()
            if h == way:
                hop(far, h, way).start()
            pass_on(far - 1, h, way).start()
    for h in (0, 1):
        hop(far, h, h).wait_recv()
        pass_on(far, h, h).start()

    def finish(k):
        for h in (0, 1):
            for way in (0, 1):
                hop(k + 1, h, way).wait_send()
                pass_on(k + 1, h, way).wait()

    loop(far - 1, finish)
    for h in (0, 1):
        hop(far, h, h).wait_send()
        pass_on(far, h, h).wait()
        pass_on(0, h, 0, own(h)).wait()
    for c in keep:
        c.wait()
    loop(members - 1, lambda k: share(k).wait())


def weights(weight, part, owners, members, call):
    depth, width = weight.shape
    steps = owners // 4 + 1
    return pl.pallas_call(
        functools.partial(weight_kernel, owners, members),
        out_shape=[
            jax.ShapeDtypeStruct((depth, owners * width), weight.dtype),
            jax.ShapeDtypeStruct((members * part.shape[0], part.shape[1]), part.dtype),
        ],
        in_specs=[VMEM] * 2,
        out_specs=[ANY] * 2,
        scratch_shapes=[
            pltpu.SemaphoreType.DMA((steps, 2, 2)),
            pltpu.SemaphoreType.DMA((steps, 2, 2)),
            pltpu.SemaphoreType.DMA((steps, 2, 2)),
            pltpu.SemaphoreType.DMA((steps, 2, 2)),
            pltpu.SemaphoreType.DMA((members,)),
            pltpu.SemaphoreType.DMA((members,)),
            pltpu.SemaphoreType.DMA((2,)),
        ],
        compiler_params=pltpu.CompilerParams(collective_id=call, has_side_effects=True),
    )(weight, part)


def per_device(attn_output, output_grad, adapter_ids, base_weight, adapter_down, adapter_up):
    owners, members = lax.axis_size("adapter"), lax.axis_size("tensor")
    tok_rows, width_part = attn_output.shape
    capacity = 5 * tok_rows // (2 * owners)
    slots = owners * capacity
    per_owner = adapter_down.shape[1] // ADAPTER_RANK
    lanes = 128

    def pack(a):
        return a.reshape(slots * width_part // lanes, lanes)

    def unpack(a):
        return a.reshape(slots, width_part)

    owner_of = adapter_ids // per_owner
    local_of = adapter_ids % per_owner
    order = jnp.arange(tok_rows, dtype=jnp.int32)
    earlier = (owner_of[:, None] == owner_of[None, :]) & (order[:, None] < order[None, :])
    rank_in = jnp.sum(earlier.astype(jnp.int32), axis=0)
    slot_of = owner_of * capacity + rank_in
    place = jnp.arange(slots, dtype=jnp.int32)[:, None] == slot_of[None, :]
    place_half = place.astype(jnp.bfloat16)
    marks = jnp.sum(jnp.where(place, (local_of + 1)[None, :], 0), axis=1).reshape(owners, capacity)
    marks = jnp.pad(marks.astype(jnp.bfloat16), ((0, 0), (0, lanes - capacity)))
    send_inputs = dot(place_half, attn_output, ((1,), (0,))).astype(jnp.bfloat16)
    recv_inputs, full_grad = first(pack(send_inputs), output_grad, owners, 1)
    recv_inputs = unpack(recv_inputs)

    grad_part = lax.dynamic_slice_in_dim(full_grad, lax.axis_index("tensor") * width_part, width_part, 1)
    send_grads = dot(place_half, grad_part, ((1,), (0,))).astype(jnp.bfloat16)
    recv_grads, all_marks = swap_labels(pack(send_grads), marks, owners, members, 2)
    recv_grads = unpack(recv_grads)
    recv_marks = lax.dynamic_slice_in_dim(
        all_marks.reshape(owners, owners, lanes), lax.axis_index("adapter"), 1, 1
    )[:, 0, :capacity].reshape(1, slots)

    adapter_of_row = jnp.arange(per_owner * ADAPTER_RANK, dtype=jnp.int32)[:, None] // ADAPTER_RANK
    spread = recv_marks.astype(jnp.float32) == (adapter_of_row + 1).astype(jnp.float32)

    def fold(a):
        return jnp.where(spread, a, 0.0).reshape(per_owner, ADAPTER_RANK, slots).sum(axis=0)

    low = jnp.concatenate(
        [
            fold(dot(adapter_down, recv_inputs, ((0,), (1,)))),
            fold(dot(adapter_up, recv_grads, ((1,), (1,)))),
        ],
        axis=0,
    )
    full_weight, low_parts = weights(base_weight, low, owners, members, 3)
    low = low_parts.reshape(members, 2 * ADAPTER_RANK, slots).sum(axis=0)
    low = (ADAPTER_SCALE * low).astype(jnp.bfloat16)

    def widen(a):
        return jnp.where(spread, jnp.tile(a, (per_owner, 1)), jnp.zeros((), jnp.bfloat16))

    up_wide, wide_gradient = widen(low[:ADAPTER_RANK]), widen(low[ADAPTER_RANK:])
    adapter_block = dot(wide_gradient, adapter_down, ((0,), (1,))).astype(jnp.bfloat16)
    returned, frozen_gradient = last(pack(adapter_block), full_grad, full_weight, owners, 4)
    returned = unpack(returned)
    down_grad = dot(recv_inputs, wide_gradient, ((0,), (1,)))
    up_grad = dot(up_wide, recv_grads, ((1,), (0,)))
    adapter_contribution = dot(place_half, returned, ((0,), (0,)))
    attention_output_gradient = (frozen_gradient + adapter_contribution).astype(jnp.bfloat16)
    return (attention_output_gradient, down_grad, up_grad)


def solution(mesh):
    placed = (
        P("adapter", "tensor"),
        P(("adapter", "tensor"), None),
        P("adapter"),
        P("tensor", "adapter"),
        P("tensor", "adapter"),
        P("adapter", "tensor"),
    )
    return jax.shard_map(
        per_device,
        mesh=mesh,
        in_specs=placed,
        out_specs=(P("adapter", "tensor"), P("tensor", "adapter"), P("adapter", "tensor")),
        check_vma=False,
    )
```

```python
import functools

import jax
import jax.numpy as jnp
from jax import lax
from jax.experimental import pallas as pl
from jax.experimental.pallas import tpu as pltpu
from jax.sharding import PartitionSpec as P

ADAPTER_RANK = 16
ADAPTER_SCALE = 2.0
MESH = pl.DeviceIdType.MESH
ANY = pl.BlockSpec(memory_space=pl.ANY)
VMEM = pl.BlockSpec(memory_space=pltpu.VMEM)
SIDE = 4


def remote(src, dst, send_sem, recv_sem, **where):
    return pltpu.make_async_remote_copy(
        src_ref=src,
        dst_ref=dst,
        send_sem=send_sem,
        recv_sem=recv_sem,
        device_id=where,
        device_id_type=MESH,
    )


def partner(q, chips):
    me = lax.axis_index("adapter")
    z, core = me // 2, me % 2
    i, flip = q // 2, (q + 1) % 2
    half = chips // 2
    shift = half + (1 - 2 * (i % 2)) * ((i + 1) // 2)
    return ((z + shift) % chips) * 2 + (core + flip) % 2


def dot(a, b, dims):
    return lax.dot_general(a, b, (dims, ((), ())), preferred_element_type=jnp.float32)


def signal(barrier, **where):
    pl.semaphore_signal(barrier, inc=1, device_id=where, device_id_type=MESH)


def loop(n, body):
    def step(k, carry):
        body(k)
        return carry

    lax.fori_loop(0, n, step, 0)


def exchange(owners, rows, src, dst, send_sem, recv_sem):
    me = lax.axis_index("adapter")

    def copy(q):
        to = partner(q, owners // 2)
        return remote(
            src.at[pl.ds(pl.multiple_of(to * rows, rows), rows)],
            dst.at[pl.ds(pl.multiple_of(me * rows, rows), rows)],
            send_sem.at[q],
            recv_sem.at[q],
            adapter=to,
        )

    return copy


def own_block(rows, src, dst, sem):
    me = lax.axis_index("adapter")
    mine = pl.ds(pl.multiple_of(me * rows, rows), rows)
    return pltpu.make_async_copy(src.at[mine], dst.at[mine], sem)


def greet_owners(owners, barrier):
    loop(owners - 1, lambda q: signal(barrier, adapter=partner(q, owners // 2)))


def label_kernel(
    owners, members, rows, src, marks, dst, marks_out,
    send_sem, recv_sem, away_send, away_recv, near_send, near_recv, own_sem,
):
    me, t = lax.axis_index("adapter"), lax.axis_index("tensor")
    chips = owners // 2
    z, core = me // 2, me % 2
    above, below = (z + t) % chips, (z + chips - t) % chips
    depth = marks.shape[0]

    barrier = pltpu.get_barrier_semaphore()
    greet_owners(owners, barrier)
    loop(members - 1, lambda k: signal(barrier, tensor=(t + k + 1) % members))
    pl.semaphore_wait(barrier, owners + members - 2)

    def block(first, blocks):
        return marks_out.at[pl.ds(pl.multiple_of(first * depth, depth), blocks * depth)]

    def away(flip):
        return remote(
            marks, block(me, 1), away_send.at[flip], away_recv.at[flip], adapter=above * 2 + (core + flip) % 2
        )

    def near(k):
        to = (t + k + 1) % members
        pair = block(below * 2, 2)
        return remote(pair, pair, near_send.at[k], near_recv.at[k], tensor=to)

    keep = pltpu.make_async_copy(marks, block(me, 1), own_sem.at[1])

    @pl.when(t == 0)
    def _():
        keep.start()

    @pl.when(t > 0)
    def _():
        away(0).start()

    away(1).start()
    copy = exchange(owners, rows, src, dst, send_sem, recv_sem)
    loop(owners - 1, lambda q: copy(q).start())
    own = own_block(rows, src, dst, own_sem.at[0])
    own.start()

    @pl.when(t == 0)
    def _():
        keep.wait()

    @pl.when(t > 0)
    def _():
        away(0).wait()

    away(1).wait()
    loop(members - 1, lambda k: near(k).start())
    own.wait()
    loop(members - 1, lambda k: near(k).wait())
    loop(owners - 1, lambda q: copy(q).wait())


def swap_labels(slots, marks, owners, members, call):
    return pl.pallas_call(
        functools.partial(label_kernel, owners, members, slots.shape[0] // owners),
        out_shape=[
            jax.ShapeDtypeStruct(slots.shape, slots.dtype),
            jax.ShapeDtypeStruct((owners * marks.shape[0], marks.shape[1]), marks.dtype),
        ],
        in_specs=[VMEM] * 2,
        out_specs=[ANY] * 2,
        scratch_shapes=[
            pltpu.SemaphoreType.DMA((owners,)),
            pltpu.SemaphoreType.DMA((owners,)),
            pltpu.SemaphoreType.DMA((2,)),
            pltpu.SemaphoreType.DMA((2,)),
            pltpu.SemaphoreType.DMA((members,)),
            pltpu.SemaphoreType.DMA((members,)),
            pltpu.SemaphoreType.DMA((2,)),
        ],
        compiler_params=pltpu.CompilerParams(collective_id=call, has_side_effects=True),
    )(slots, marks)


def last_kernel(
    owners, rows, src, grad, weight, dst, product, send_sem, recv_sem, own_sem, grad_held, weight_held, load_sem,
):
    barrier = pltpu.get_barrier_semaphore()
    greet_owners(owners, barrier)
    pl.semaphore_wait(barrier, owners - 1)
    copy = exchange(owners, rows, src, dst, send_sem, recv_sem)
    loop(owners - 1, lambda q: copy(q).start())
    own = own_block(rows, src, dst, own_sem)
    own.start()
    steps = load_sem.shape[0]
    width = grad.shape[1] // steps

    def part(k):
        return pl.ds(pl.multiple_of(k * width, width), width)

    def load(k):
        return (
            pltpu.make_async_copy(grad.at[:, part(k)], grad_held.at[:, part(k)], load_sem.at[k, 0]),
            pltpu.make_async_copy(weight.at[:, part(k)], weight_held.at[:, part(k)], load_sem.at[k, 1]),
        )

    def fetch(k):
        for c in load(k):
            c.start()

    def step(k):
        for c in load(k):
            c.wait()
        product[...] += dot(grad_held[:, part(k)], weight_held[:, part(k)], ((1,), (1,)))

    loop(steps, fetch)
    product[...] = jnp.zeros_like(product)
    loop(steps, step)
    own.wait()
    loop(owners - 1, lambda q: copy(q).wait())


def last(slots, grad, weight, owners, call):
    steps = 8
    return pl.pallas_call(
        functools.partial(last_kernel, owners, slots.shape[0] // owners),
        out_shape=[
            jax.ShapeDtypeStruct(slots.shape, slots.dtype),
            jax.ShapeDtypeStruct((grad.shape[0], weight.shape[0]), jnp.float32),
        ],
        in_specs=[VMEM, ANY, ANY],
        out_specs=[ANY, VMEM],
        scratch_shapes=[
            pltpu.SemaphoreType.DMA((owners,)),
            pltpu.SemaphoreType.DMA((owners,)),
            pltpu.SemaphoreType.DMA,
            pltpu.VMEM(grad.shape, grad.dtype),
            pltpu.VMEM(weight.shape, weight.dtype),
            pltpu.SemaphoreType.DMA((steps, 2)),
        ],
        compiler_params=pltpu.CompilerParams(
            collective_id=call, has_side_effects=True, vmem_limit_bytes=63 * 1024 * 1024
        ),
    )(slots, grad, weight)


def first_kernel(
    owners, rows, src, grad, dst, full, send_sem, recv_sem, own_sem, ring_send, ring_recv,
):
    t = lax.axis_index("tensor")
    x, y = t // SIDE, t % SIDE
    tokens, width = grad.shape
    half, quarter = width // 2, width // 4

    def at(x_at, y_at):
        return (x_at % SIDE) * SIDE + y_at % SIDE

    barrier = pltpu.get_barrier_semaphore()
    greet_owners(owners, barrier)
    for dx, dy in ((1, 0), (3, 0), (0, 1), (0, 3)):
        signal(barrier, tensor=at(x + dx, y + dy))
    pl.semaphore_wait(barrier, owners + 3)

    copy = exchange(owners, rows, src, dst, send_sem, recv_sem)

    def cut(block, first, size):
        return full.at[pl.ds(pl.multiple_of(block * tokens, tokens), tokens), pl.ds(first, size)]

    def mine(first, size):
        return grad.at[:, pl.ds(first, size)]

    started = []

    def send(src_ref, block, first, size, sem, to):
        c = remote(src_ref, cut(block, first, size), ring_send.at[sem], ring_recv.at[sem], tensor=to)
        c.start()
        started.append(c)
        return c

    def along(side, d, e):
        return at(x + d, y + e) if side == 0 else at(x + e, y + d)

    first_hop, second = [], [[], []]
    for side in (0, 1):
        base = side * half
        first_hop.append(
            [
                send(mine(base, half), t, base, half, side * 20, along(side, 1, 0)),
                send(mine(base, half), t, base, half, side * 20 + 1, along(side, 3, 0)),
            ]
        )
    for side in (0, 1):
        base = side * half
        second[side].append(
            [
                send(mine(base, half), t, base, half, side * 20 + 4, along(side, 0, 1)),
                send(mine(base, half), t, base, half, side * 20 + 5, along(side, 0, 3)),
            ]
        )
    loop(owners - 1, lambda q: copy(q).start())
    own = [
        own_block(rows, src, dst, own_sem.at[0]),
        pltpu.make_async_copy(grad, cut(t, 0, width), own_sem.at[1]),
    ]
    for c in own:
        c.start()
    last_hop = []
    for side in (0, 1):
        base, sem = side * half, side * 20
        a, b = first_hop[side]
        a.wait_recv()
        from_a = along(side, 3, 0)
        f1 = send(cut(from_a, base, quarter), from_a, base, quarter, sem + 2, along(side, 1, 0))
        b.wait_recv()
        from_b = along(side, 1, 0)
        f2 = send(cut(from_b, base + quarter, quarter), from_b, base + quarter, quarter, sem + 3, along(side, 3, 0))
        last_hop.append((f1, f2))
        for j, block in ((1, from_a), (2, from_b)):
            second[side].append(
                [
                    send(cut(block, base, half), block, base, half, sem + 4 + 4 * j, along(side, 0, 1)),
                    send(cut(block, base, half), block, base, half, sem + 5 + 4 * j, along(side, 0, 3)),
                ]
            )
    for side in (0, 1):
        base, sem = side * half, side * 20
        for c in last_hop[side]:
            c.wait_recv()
        block = along(side, 2, 0)
        second[side].append(
            [
                send(cut(block, base, half), block, base, half, sem + 16, along(side, 0, 1)),
                send(cut(block, base, half), block, base, half, sem + 17, along(side, 0, 3)),
            ]
        )
    final = []
    for j in range(4):
        for side in (0, 1):
            base, sem = side * half, side * 20
            d = (0, 3, 1, 2)[j]
            a, b = second[side][j]
            a.wait_recv()
            block = along(side, d, 3)
            final.append(
                send(cut(block, base, quarter), block, base, quarter, sem + 6 + 4 * j, along(side, 0, 1))
            )
            b.wait_recv()
            block = along(side, d, 1)
            final.append(
                send(
                    cut(block, base + quarter, quarter), block, base + quarter, quarter,
                    sem + 7 + 4 * j, along(side, 0, 3),
                )
            )
    for c in final:
        c.wait_recv()
    for c in started:
        c.wait_send()
    for c in own:
        c.wait()
    loop(owners - 1, lambda q: copy(q).wait())


def first(slots, grad, owners, call):
    members = SIDE * SIDE
    tokens, width = grad.shape
    return pl.pallas_call(
        functools.partial(first_kernel, owners, slots.shape[0] // owners),
        out_shape=[
            jax.ShapeDtypeStruct(slots.shape, slots.dtype),
            jax.ShapeDtypeStruct((members * tokens, width), grad.dtype),
        ],
        in_specs=[VMEM] * 2,
        out_specs=[ANY] * 2,
        scratch_shapes=[
            pltpu.SemaphoreType.DMA((owners,)),
            pltpu.SemaphoreType.DMA((owners,)),
            pltpu.SemaphoreType.DMA((2,)),
            pltpu.SemaphoreType.DMA((40,)),
            pltpu.SemaphoreType.DMA((40,)),
        ],
        compiler_params=pltpu.CompilerParams(collective_id=call, has_side_effects=True),
    )(slots, grad)


def weight_kernel(
    owners, members, weight, part, full, parts, ring_send, ring_recv, twin_send, twin_recv, part_send, part_recv, own_sem,
):
    chips = owners // 2
    me, t = lax.axis_index("adapter"), lax.axis_index("tensor")
    z, core = me // 2, me % 2
    depth, width = weight.shape
    rows = depth // 2
    right, left, twin = ((z + 1) % chips) * 2 + core, ((z + chips - 1) % chips) * 2 + core, z * 2 + 1 - core
    part_rows = part.shape[0]
    far = chips // 2

    barrier = pltpu.get_barrier_semaphore()
    for to in (right, left, twin):
        signal(barrier, adapter=to)
    loop(members - 1, lambda k: signal(barrier, tensor=(t + k + 1) % members))
    pl.semaphore_wait(barrier, members + 2)

    def cut(chip, h):
        column = pl.multiple_of(((chip % chips) * 2 + core) * width, width)
        return full.at[pl.ds(h * rows, rows), pl.ds(column, width)]

    def hop(s, h, way, src=None):
        chip = z + chips - s + 1 if way == 0 else z + s - 1
        return remote(
            cut(chip, h) if src is None else src,
            cut(chip, h),
            ring_send.at[s, h, way],
            ring_recv.at[s, h, way],
            adapter=right if way == 0 else left,
        )

    def pass_on(s, h, way, src=None):
        chip = z + chips - s if way == 0 else z + s
        return remote(
            cut(chip, h) if src is None else src,
            cut(chip, h),
            twin_send.at[s, h, way],
            twin_recv.at[s, h, way],
            adapter=twin,
        )

    def share(k):
        to = (t + k + 1) % members
        return remote(
            part,
            parts.at[pl.ds(pl.multiple_of(t * part_rows, part_rows), part_rows)],
            part_send.at[k],
            part_recv.at[k],
            tensor=to,
        )

    def own(h):
        return weight.at[pl.ds(h * rows, rows)]

    loop(members - 1, lambda k: share(k).start())
    for h in (0, 1):
        for way in (0, 1):
            hop(1, h, way, own(h)).start()
    for h in (0, 1):
        pass_on(0, h, 0, own(h)).start()
    keep = [
        pltpu.make_async_copy(weight, full.at[:, pl.ds(pl.multiple_of(me * width, width), width)], own_sem.at[0]),
        pltpu.make_async_copy(
            part, parts.at[pl.ds(pl.multiple_of(t * part_rows, part_rows), part_rows)], own_sem.at[1]
        ),
    ]
    for c in keep:
        c.start()

    def step(s):
        for h in (0, 1):
            for way in (0, 1):
                hop(s - 1, h, way).wait_recv()
                hop(s, h, way).start()
                pass_on(s - 1, h, way).start()

    loop(far - 2, lambda k: step(k + 2))
    for h in (0, 1):
        for way in (0, 1):
            hop(far - 1, h, way).wait_recv()
            if h == way:
                hop(far, h, way).start()
            pass_on(far - 1, h, way).start()
    for h in (0, 1):
        hop(far, h, h).wait_recv()
        pass_on(far, h, h).start()

    def finish(k):
        for h in (0, 1):
            for way in (0, 1):
                hop(k + 1, h, way).wait_send()
                pass_on(k + 1, h, way).wait()

    loop(far - 1, finish)
    for h in (0, 1):
        hop(far, h, h).wait_send()
        pass_on(far, h, h).wait()
        pass_on(0, h, 0, own(h)).wait()
    for c in keep:
        c.wait()
    loop(members - 1, lambda k: share(k).wait())


def weights(weight, part, owners, members, call):
    depth, width = weight.shape
    steps = owners // 4 + 1
    return pl.pallas_call(
        functools.partial(weight_kernel, owners, members),
        out_shape=[
            jax.ShapeDtypeStruct((depth, owners * width), weight.dtype),
            jax.ShapeDtypeStruct((members * part.shape[0], part.shape[1]), part.dtype),
        ],
        in_specs=[VMEM] * 2,
        out_specs=[ANY] * 2,
        scratch_shapes=[
            pltpu.SemaphoreType.DMA((steps, 2, 2)),
            pltpu.SemaphoreType.DMA((steps, 2, 2)),
            pltpu.SemaphoreType.DMA((steps, 2, 2)),
            pltpu.SemaphoreType.DMA((steps, 2, 2)),
            pltpu.SemaphoreType.DMA((members,)),
            pltpu.SemaphoreType.DMA((members,)),
            pltpu.SemaphoreType.DMA((2,)),
        ],
        compiler_params=pltpu.CompilerParams(collective_id=call, has_side_effects=True),
    )(weight, part)


def per_device(attn_output, output_grad, adapter_ids, base_weight, adapter_down, adapter_up):
    owners, members = lax.axis_size("adapter"), lax.axis_size("tensor")
    tok_rows, width_part = attn_output.shape
    capacity = 5 * tok_rows // (2 * owners)
    slots = owners * capacity
    per_owner = adapter_down.shape[1] // ADAPTER_RANK
    lanes = 128

    def pack(a):
        return a.reshape(slots * width_part // lanes, lanes)

    def unpack(a):
        return a.reshape(slots, width_part)

    owner_of = adapter_ids // per_owner
    local_of = adapter_ids % per_owner
    order = jnp.arange(tok_rows, dtype=jnp.int32)
    earlier = (owner_of[:, None] == owner_of[None, :]) & (order[:, None] < order[None, :])
    rank_in = jnp.sum(earlier.astype(jnp.int32), axis=0)
    slot_of = owner_of * capacity + rank_in
    place = jnp.arange(slots, dtype=jnp.int32)[:, None] == slot_of[None, :]
    place_half = place.astype(jnp.bfloat16)
    marks = jnp.sum(jnp.where(place, (local_of + 1)[None, :], 0), axis=1).reshape(owners, capacity)
    marks = jnp.pad(marks.astype(jnp.bfloat16), ((0, 0), (0, lanes - capacity)))
    send_inputs = dot(place_half, attn_output, ((1,), (0,))).astype(jnp.bfloat16)
    recv_inputs, full_grad = first(pack(send_inputs), output_grad, owners, 1)
    recv_inputs = unpack(recv_inputs)

    grad_part = lax.dynamic_slice_in_dim(full_grad, lax.axis_index("tensor") * width_part, width_part, 1)
    send_grads = dot(place_half, grad_part, ((1,), (0,))).astype(jnp.bfloat16)
    recv_grads, all_marks = swap_labels(pack(send_grads), marks, owners, members, 2)
    recv_grads = unpack(recv_grads)
    recv_marks = lax.dynamic_slice_in_dim(
        all_marks.reshape(owners, owners, lanes), lax.axis_index("adapter"), 1, 1
    )[:, 0, :capacity].reshape(1, slots)

    adapter_of_row = jnp.arange(per_owner * ADAPTER_RANK, dtype=jnp.int32)[:, None] // ADAPTER_RANK
    spread = recv_marks.astype(jnp.float32) == (adapter_of_row + 1).astype(jnp.float32)

    def fold(a):
        return jnp.where(spread, a, 0.0).reshape(per_owner, ADAPTER_RANK, slots).sum(axis=0)

    low = jnp.concatenate(
        [
            fold(dot(adapter_down, recv_inputs, ((0,), (1,)))),
            fold(dot(adapter_up, recv_grads, ((1,), (1,)))),
        ],
        axis=0,
    )
    full_weight, low_parts = weights(base_weight, low, owners, members, 3)
    low = low_parts.reshape(members, 2 * ADAPTER_RANK, slots).sum(axis=0)
    low = (ADAPTER_SCALE * low).astype(jnp.bfloat16)

    def widen(a):
        return jnp.where(spread, jnp.tile(a, (per_owner, 1)), jnp.zeros((), jnp.bfloat16))

    up_wide, wide_gradient = widen(low[:ADAPTER_RANK]), widen(low[ADAPTER_RANK:])
    adapter_block = dot(wide_gradient, adapter_down, ((0,), (1,))).astype(jnp.bfloat16)
    returned, frozen_gradient = last(pack(adapter_block), full_grad, full_weight, owners, 4)
    returned = unpack(returned)
    down_grad = dot(recv_inputs, wide_gradient, ((0,), (1,)))
    up_grad = dot(up_wide, recv_grads, ((1,), (0,)))
    adapter_contribution = dot(place_half, returned, ((0,), (0,)))
    attention_output_gradient = (frozen_gradient + adapter_contribution).astype(jnp.bfloat16)
    return (attention_output_gradient, down_grad, up_grad)


def solution(mesh):
    placed = (
        P("adapter", "tensor"),
        P(("adapter", "tensor"), None),
        P("adapter"),
        P("tensor", "adapter"),
        P("tensor", "adapter"),
        P("adapter", "tensor"),
    )
    return jax.shard_map(
        per_device,
        mesh=mesh,
        in_specs=placed,
        out_specs=(P("adapter", "tensor"), P("tensor", "adapter"), P("adapter", "tensor")),
        check_vma=False,
    )
```

```python
import functools

import jax
import jax.numpy as jnp
from jax import lax
from jax.experimental import pallas as pl
from jax.experimental.pallas import tpu as pltpu
from jax.sharding import PartitionSpec as P

ADAPTER_RANK = 16
ADAPTER_SCALE = 2.0
MESH = pl.DeviceIdType.MESH
ANY = pl.BlockSpec(memory_space=pl.ANY)
VMEM = pl.BlockSpec(memory_space=pltpu.VMEM)
SIDE = 4


def remote(src, dst, send_sem, recv_sem, **where):
    return pltpu.make_async_remote_copy(
        src_ref=src,
        dst_ref=dst,
        send_sem=send_sem,
        recv_sem=recv_sem,
        device_id=where,
        device_id_type=MESH,
    )


def partner(q, chips):
    me = lax.axis_index("adapter")
    z, core = me // 2, me % 2
    i, flip = q // 2, (q + 1) % 2
    half = chips // 2
    shift = half + (1 - 2 * (i % 2)) * ((i + 1) // 2)
    return ((z + shift) % chips) * 2 + (core + flip) % 2


def dot(a, b, dims):
    return lax.dot_general(a, b, (dims, ((), ())), preferred_element_type=jnp.float32)


def signal(barrier, **where):
    pl.semaphore_signal(barrier, inc=1, device_id=where, device_id_type=MESH)


def loop(n, body):
    def step(k, carry):
        body(k)
        return carry

    lax.fori_loop(0, n, step, 0)


def exchange(owners, rows, src, dst, send_sem, recv_sem):
    me = lax.axis_index("adapter")

    def copy(q):
        to = partner(q, owners // 2)
        return remote(
            src.at[pl.ds(pl.multiple_of(to * rows, rows), rows)],
            dst.at[pl.ds(pl.multiple_of(me * rows, rows), rows)],
            send_sem.at[q],
            recv_sem.at[q],
            adapter=to,
        )

    return copy


def own_block(rows, src, dst, sem):
    me = lax.axis_index("adapter")
    mine = pl.ds(pl.multiple_of(me * rows, rows), rows)
    return pltpu.make_async_copy(src.at[mine], dst.at[mine], sem)


def greet_owners(owners, barrier):
    loop(owners - 1, lambda q: signal(barrier, adapter=partner(q, owners // 2)))


def label_kernel(
    owners, members, rows, src, marks, dst, marks_out,
    send_sem, recv_sem, away_send, away_recv, near_send, near_recv, own_sem,
):
    me, t = lax.axis_index("adapter"), lax.axis_index("tensor")
    chips = owners // 2
    z, core = me // 2, me % 2
    above, below = (z + t) % chips, (z + chips - t) % chips
    depth = marks.shape[0]

    barrier = pltpu.get_barrier_semaphore()
    greet_owners(owners, barrier)
    loop(members - 1, lambda k: signal(barrier, tensor=(t + k + 1) % members))
    pl.semaphore_wait(barrier, owners + members - 2)

    def block(first, blocks):
        return marks_out.at[pl.ds(pl.multiple_of(first * depth, depth), blocks * depth)]

    def away(flip):
        return remote(
            marks, block(me, 1), away_send.at[flip], away_recv.at[flip], adapter=above * 2 + (core + flip) % 2
        )

    def near(k):
        to = (t + k + 1) % members
        pair = block(below * 2, 2)
        return remote(pair, pair, near_send.at[k], near_recv.at[k], tensor=to)

    keep = pltpu.make_async_copy(marks, block(me, 1), own_sem.at[1])

    @pl.when(t == 0)
    def _():
        keep.start()

    @pl.when(t > 0)
    def _():
        away(0).start()

    away(1).start()
    copy = exchange(owners, rows, src, dst, send_sem, recv_sem)
    loop(owners - 1, lambda q: copy(q).start())
    own = own_block(rows, src, dst, own_sem.at[0])
    own.start()

    @pl.when(t == 0)
    def _():
        keep.wait()

    @pl.when(t > 0)
    def _():
        away(0).wait()

    away(1).wait()
    loop(members - 1, lambda k: near(k).start())
    own.wait()
    loop(members - 1, lambda k: near(k).wait())
    loop(owners - 1, lambda q: copy(q).wait())


def swap_labels(slots, marks, owners, members, call):
    return pl.pallas_call(
        functools.partial(label_kernel, owners, members, slots.shape[0] // owners),
        out_shape=[
            jax.ShapeDtypeStruct(slots.shape, slots.dtype),
            jax.ShapeDtypeStruct((owners * marks.shape[0], marks.shape[1]), marks.dtype),
        ],
        in_specs=[VMEM] * 2,
        out_specs=[ANY] * 2,
        scratch_shapes=[
            pltpu.SemaphoreType.DMA((owners,)),
            pltpu.SemaphoreType.DMA((owners,)),
            pltpu.SemaphoreType.DMA((2,)),
            pltpu.SemaphoreType.DMA((2,)),
            pltpu.SemaphoreType.DMA((members,)),
            pltpu.SemaphoreType.DMA((members,)),
            pltpu.SemaphoreType.DMA((2,)),
        ],
        compiler_params=pltpu.CompilerParams(collective_id=call, has_side_effects=True),
    )(slots, marks)


def last_kernel(
    owners, rows, src, grad, weight, dst, product, send_sem, recv_sem, own_sem, grad_held, weight_held, load_sem,
):
    barrier = pltpu.get_barrier_semaphore()
    greet_owners(owners, barrier)
    pl.semaphore_wait(barrier, owners - 1)
    copy = exchange(owners, rows, src, dst, send_sem, recv_sem)
    loop(owners - 1, lambda q: copy(q).start())
    own = own_block(rows, src, dst, own_sem)
    own.start()
    steps = load_sem.shape[0]
    width = grad.shape[1] // steps

    def part(k):
        return pl.ds(pl.multiple_of(k * width, width), width)

    def load(k):
        return (
            pltpu.make_async_copy(grad.at[:, part(k)], grad_held.at[:, part(k)], load_sem.at[k, 0]),
            pltpu.make_async_copy(weight.at[:, part(k)], weight_held.at[:, part(k)], load_sem.at[k, 1]),
        )

    def fetch(k):
        for c in load(k):
            c.start()

    def step(k):
        for c in load(k):
            c.wait()
        product[...] += dot(grad_held[:, part(k)], weight_held[:, part(k)], ((1,), (1,)))

    loop(steps, fetch)
    product[...] = jnp.zeros_like(product)
    loop(steps, step)
    own.wait()
    loop(owners - 1, lambda q: copy(q).wait())


def last(slots, grad, weight, owners, call):
    steps = 8
    return pl.pallas_call(
        functools.partial(last_kernel, owners, slots.shape[0] // owners),
        out_shape=[
            jax.ShapeDtypeStruct(slots.shape, slots.dtype),
            jax.ShapeDtypeStruct((grad.shape[0], weight.shape[0]), jnp.float32),
        ],
        in_specs=[VMEM, ANY, ANY],
        out_specs=[ANY, VMEM],
        scratch_shapes=[
            pltpu.SemaphoreType.DMA((owners,)),
            pltpu.SemaphoreType.DMA((owners,)),
            pltpu.SemaphoreType.DMA,
            pltpu.VMEM(grad.shape, grad.dtype),
            pltpu.VMEM(weight.shape, weight.dtype),
            pltpu.SemaphoreType.DMA((steps, 2)),
        ],
        compiler_params=pltpu.CompilerParams(
            collective_id=call, has_side_effects=True, vmem_limit_bytes=121 * 512 * 1024
        ),
    )(slots, grad, weight)


def first_kernel(
    owners, rows, src, grad, dst, full, send_sem, recv_sem, own_sem, ring_send, ring_recv,
):
    t = lax.axis_index("tensor")
    x, y = t // SIDE, t % SIDE
    tokens, width = grad.shape
    half, quarter = width // 2, width // 4

    def at(x_at, y_at):
        return (x_at % SIDE) * SIDE + y_at % SIDE

    barrier = pltpu.get_barrier_semaphore()
    greet_owners(owners, barrier)
    for dx, dy in ((1, 0), (3, 0), (0, 1), (0, 3)):
        signal(barrier, tensor=at(x + dx, y + dy))
    pl.semaphore_wait(barrier, owners + 3)

    copy = exchange(owners, rows, src, dst, send_sem, recv_sem)

    def cut(block, first, size):
        return full.at[pl.ds(pl.multiple_of(block * tokens, tokens), tokens), pl.ds(first, size)]

    def mine(first, size):
        return grad.at[:, pl.ds(first, size)]

    started = []

    def send(src_ref, block, first, size, sem, to):
        c = remote(src_ref, cut(block, first, size), ring_send.at[sem], ring_recv.at[sem], tensor=to)
        c.start()
        started.append(c)
        return c

    def along(side, d, e):
        return at(x + d, y + e) if side == 0 else at(x + e, y + d)

    first_hop, second = [], [[], []]
    for side in (0, 1):
        base = side * half
        first_hop.append(
            [
                send(mine(base, half), t, base, half, side * 20, along(side, 1, 0)),
                send(mine(base, half), t, base, half, side * 20 + 1, along(side, 3, 0)),
            ]
        )
    for side in (0, 1):
        base = side * half
        second[side].append(
            [
                send(mine(base, half), t, base, half, side * 20 + 4, along(side, 0, 1)),
                send(mine(base, half), t, base, half, side * 20 + 5, along(side, 0, 3)),
            ]
        )
    loop(owners - 1, lambda q: copy(q).start())
    own = [
        own_block(rows, src, dst, own_sem.at[0]),
        pltpu.make_async_copy(grad, cut(t, 0, width), own_sem.at[1]),
    ]
    for c in own:
        c.start()
    last_hop = []
    for side in (0, 1):
        base, sem = side * half, side * 20
        a, b = first_hop[side]
        a.wait_recv()
        from_a = along(side, 3, 0)
        f1 = send(cut(from_a, base, quarter), from_a, base, quarter, sem + 2, along(side, 1, 0))
        b.wait_recv()
        from_b = along(side, 1, 0)
        f2 = send(cut(from_b, base + quarter, quarter), from_b, base + quarter, quarter, sem + 3, along(side, 3, 0))
        last_hop.append((f1, f2))
        for j, block in ((1, from_a), (2, from_b)):
            second[side].append(
                [
                    send(cut(block, base, half), block, base, half, sem + 4 + 4 * j, along(side, 0, 1)),
                    send(cut(block, base, half), block, base, half, sem + 5 + 4 * j, along(side, 0, 3)),
                ]
            )
    for side in (0, 1):
        base, sem = side * half, side * 20
        for c in last_hop[side]:
            c.wait_recv()
        block = along(side, 2, 0)
        second[side].append(
            [
                send(cut(block, base, half), block, base, half, sem + 16, along(side, 0, 1)),
                send(cut(block, base, half), block, base, half, sem + 17, along(side, 0, 3)),
            ]
        )
    final = []
    for j in range(4):
        for side in (0, 1):
            base, sem = side * half, side * 20
            d = (0, 3, 1, 2)[j]
            a, b = second[side][j]
            a.wait_recv()
            block = along(side, d, 3)
            final.append(
                send(cut(block, base, quarter), block, base, quarter, sem + 6 + 4 * j, along(side, 0, 1))
            )
            b.wait_recv()
            block = along(side, d, 1)
            final.append(
                send(
                    cut(block, base + quarter, quarter), block, base + quarter, quarter,
                    sem + 7 + 4 * j, along(side, 0, 3),
                )
            )
    for c in final:
        c.wait_recv()
    for c in started:
        c.wait_send()
    for c in own:
        c.wait()
    loop(owners - 1, lambda q: copy(q).wait())


def first(slots, grad, owners, call):
    members = SIDE * SIDE
    tokens, width = grad.shape
    return pl.pallas_call(
        functools.partial(first_kernel, owners, slots.shape[0] // owners),
        out_shape=[
            jax.ShapeDtypeStruct(slots.shape, slots.dtype),
            jax.ShapeDtypeStruct((members * tokens, width), grad.dtype),
        ],
        in_specs=[VMEM] * 2,
        out_specs=[ANY] * 2,
        scratch_shapes=[
            pltpu.SemaphoreType.DMA((owners,)),
            pltpu.SemaphoreType.DMA((owners,)),
            pltpu.SemaphoreType.DMA((2,)),
            pltpu.SemaphoreType.DMA((40,)),
            pltpu.SemaphoreType.DMA((40,)),
        ],
        compiler_params=pltpu.CompilerParams(collective_id=call, has_side_effects=True),
    )(slots, grad)


def weight_kernel(
    owners, members, weight, part, full, parts, ring_send, ring_recv, twin_send, twin_recv, part_send, part_recv, own_sem,
):
    chips = owners // 2
    me, t = lax.axis_index("adapter"), lax.axis_index("tensor")
    z, core = me // 2, me % 2
    depth, width = weight.shape
    rows = depth // 2
    right, left, twin = ((z + 1) % chips) * 2 + core, ((z + chips - 1) % chips) * 2 + core, z * 2 + 1 - core
    part_rows = part.shape[0]
    far = chips // 2

    barrier = pltpu.get_barrier_semaphore()
    for to in (right, left, twin):
        signal(barrier, adapter=to)
    loop(members - 1, lambda k: signal(barrier, tensor=(t + k + 1) % members))
    pl.semaphore_wait(barrier, members + 2)

    def cut(chip, h):
        column = pl.multiple_of(((chip % chips) * 2 + core) * width, width)
        return full.at[pl.ds(h * rows, rows), pl.ds(column, width)]

    def hop(s, h, way, src=None):
        chip = z + chips - s + 1 if way == 0 else z + s - 1
        return remote(
            cut(chip, h) if src is None else src,
            cut(chip, h),
            ring_send.at[s, h, way],
            ring_recv.at[s, h, way],
            adapter=right if way == 0 else left,
        )

    def pass_on(s, h, way, src=None):
        chip = z + chips - s if way == 0 else z + s
        return remote(
            cut(chip, h) if src is None else src,
            cut(chip, h),
            twin_send.at[s, h, way],
            twin_recv.at[s, h, way],
            adapter=twin,
        )

    def share(k):
        to = (t + k + 1) % members
        return remote(
            part,
            parts.at[pl.ds(pl.multiple_of(t * part_rows, part_rows), part_rows)],
            part_send.at[k],
            part_recv.at[k],
            tensor=to,
        )

    def own(h):
        return weight.at[pl.ds(h * rows, rows)]

    loop(members - 1, lambda k: share(k).start())
    for h in (0, 1):
        for way in (0, 1):
            hop(1, h, way, own(h)).start()
    for h in (0, 1):
        pass_on(0, h, 0, own(h)).start()
    keep = [
        pltpu.make_async_copy(weight, full.at[:, pl.ds(pl.multiple_of(me * width, width), width)], own_sem.at[0]),
        pltpu.make_async_copy(
            part, parts.at[pl.ds(pl.multiple_of(t * part_rows, part_rows), part_rows)], own_sem.at[1]
        ),
    ]
    for c in keep:
        c.start()

    def step(s):
        for h in (0, 1):
            for way in (0, 1):
                hop(s - 1, h, way).wait_recv()
                hop(s, h, way).start()
                pass_on(s - 1, h, way).start()

    loop(far - 2, lambda k: step(k + 2))
    for h in (0, 1):
        for way in (0, 1):
            hop(far - 1, h, way).wait_recv()
            if h == way:
                hop(far, h, way).start()
            pass_on(far - 1, h, way).start()
    for h in (0, 1):
        hop(far, h, h).wait_recv()
        pass_on(far, h, h).start()

    def finish(k):
        for h in (0, 1):
            for way in (0, 1):
                hop(k + 1, h, way).wait_send()
                pass_on(k + 1, h, way).wait()

    loop(far - 1, finish)
    for h in (0, 1):
        hop(far, h, h).wait_send()
        pass_on(far, h, h).wait()
        pass_on(0, h, 0, own(h)).wait()
    for c in keep:
        c.wait()
    loop(members - 1, lambda k: share(k).wait())


def weights(weight, part, owners, members, call):
    depth, width = weight.shape
    steps = owners // 4 + 1
    return pl.pallas_call(
        functools.partial(weight_kernel, owners, members),
        out_shape=[
            jax.ShapeDtypeStruct((depth, owners * width), weight.dtype),
            jax.ShapeDtypeStruct((members * part.shape[0], part.shape[1]), part.dtype),
        ],
        in_specs=[VMEM] * 2,
        out_specs=[ANY] * 2,
        scratch_shapes=[
            pltpu.SemaphoreType.DMA((steps, 2, 2)),
            pltpu.SemaphoreType.DMA((steps, 2, 2)),
            pltpu.SemaphoreType.DMA((steps, 2, 2)),
            pltpu.SemaphoreType.DMA((steps, 2, 2)),
            pltpu.SemaphoreType.DMA((members,)),
            pltpu.SemaphoreType.DMA((members,)),
            pltpu.SemaphoreType.DMA((2,)),
        ],
        compiler_params=pltpu.CompilerParams(collective_id=call, has_side_effects=True),
    )(weight, part)


def per_device(attn_output, output_grad, adapter_ids, base_weight, adapter_down, adapter_up):
    owners, members = lax.axis_size("adapter"), lax.axis_size("tensor")
    tok_rows, width_part = attn_output.shape
    capacity = 5 * tok_rows // (2 * owners)
    slots = owners * capacity
    per_owner = adapter_down.shape[1] // ADAPTER_RANK
    lanes = 128

    def pack(a):
        return a.reshape(slots * width_part // lanes, lanes)

    def unpack(a):
        return a.reshape(slots, width_part)

    owner_of = adapter_ids // per_owner
    local_of = adapter_ids % per_owner
    order = jnp.arange(tok_rows, dtype=jnp.int32)
    earlier = (owner_of[:, None] == owner_of[None, :]) & (order[:, None] < order[None, :])
    rank_in = jnp.sum(earlier.astype(jnp.int32), axis=0)
    slot_of = owner_of * capacity + rank_in
    place = jnp.arange(slots, dtype=jnp.int32)[:, None] == slot_of[None, :]
    place_half = place.astype(jnp.bfloat16)
    marks = jnp.sum(jnp.where(place, (local_of + 1)[None, :], 0), axis=1).reshape(owners, capacity)
    marks = jnp.pad(marks.astype(jnp.bfloat16), ((0, 0), (0, lanes - capacity)))
    send_inputs = dot(place_half, attn_output, ((1,), (0,))).astype(jnp.bfloat16)
    recv_inputs, full_grad = first(pack(send_inputs), output_grad, owners, 1)
    recv_inputs = unpack(recv_inputs)

    grad_part = lax.dynamic_slice_in_dim(full_grad, lax.axis_index("tensor") * width_part, width_part, 1)
    send_grads = dot(place_half, grad_part, ((1,), (0,))).astype(jnp.bfloat16)
    recv_grads, all_marks = swap_labels(pack(send_grads), marks, owners, members, 2)
    recv_grads = unpack(recv_grads)
    recv_marks = lax.dynamic_slice_in_dim(
        all_marks.reshape(owners, owners, lanes), lax.axis_index("adapter"), 1, 1
    )[:, 0, :capacity].reshape(1, slots)

    adapter_of_row = jnp.arange(per_owner * ADAPTER_RANK, dtype=jnp.int32)[:, None] // ADAPTER_RANK
    spread = recv_marks.astype(jnp.float32) == (adapter_of_row + 1).astype(jnp.float32)

    def fold(a):
        return jnp.where(spread, a, 0.0).reshape(per_owner, ADAPTER_RANK, slots).sum(axis=0)

    low = jnp.concatenate(
        [
            fold(dot(adapter_down, recv_inputs, ((0,), (1,)))),
            fold(dot(adapter_up, recv_grads, ((1,), (1,)))),
        ],
        axis=0,
    )
    full_weight, low_parts = weights(base_weight, low, owners, members, 3)
    low = low_parts.reshape(members, 2 * ADAPTER_RANK, slots).sum(axis=0)
    low = (ADAPTER_SCALE * low).astype(jnp.bfloat16)

    def widen(a):
        return jnp.where(spread, jnp.tile(a, (per_owner, 1)), jnp.zeros((), jnp.bfloat16))

    up_wide, wide_gradient = widen(low[:ADAPTER_RANK]), widen(low[ADAPTER_RANK:])
    adapter_block = dot(wide_gradient, adapter_down, ((0,), (1,))).astype(jnp.bfloat16)
    returned, frozen_gradient = last(pack(adapter_block), full_grad, full_weight, owners, 4)
    returned = unpack(returned)
    down_grad = dot(recv_inputs, wide_gradient, ((0,), (1,)))
    up_grad = dot(up_wide, recv_grads, ((1,), (0,)))
    adapter_contribution = dot(place_half, returned, ((0,), (0,)))
    attention_output_gradient = (frozen_gradient + adapter_contribution).astype(jnp.bfloat16)
    return (attention_output_gradient, down_grad, up_grad)


def solution(mesh):
    placed = (
        P("adapter", "tensor"),
        P(("adapter", "tensor"), None),
        P("adapter"),
        P("tensor", "adapter"),
        P("tensor", "adapter"),
        P("adapter", "tensor"),
    )
    return jax.shard_map(
        per_device,
        mesh=mesh,
        in_specs=placed,
        out_specs=(P("adapter", "tensor"), P("tensor", "adapter"), P("adapter", "tensor")),
        check_vma=False,
    )
```
